256 devices in a mesh: chan: 64 (over y, x_hi, z), hour: 4 (over x_lo, core).
Axes of the slice: x: 4 (x_hi: 2, x_lo: 2; x = x_hi * 2 + x_lo), y: 4, z: 8, core: 2. Of those that a mesh axis runs over, the one named last changes fastest.
Arguments:
- records: bfloat16 [2560, 64, 2048], P('chan', 'hour'), may hold values from -6 to 6
- live_channels: int32 [2560], P('chan'), may hold values 0 or 1
- live_windows: int32 [64], P('hour'), may hold values 0 or 1
Outputs:
- correlations: bfloat16 [2560, 2, 40, 512], P('chan', None, None, 'hour')
The draws below stay inside these ranges and needn't reach their ends.
All inputs are finite; a program needn't handle non-finite values. No bound on the sum of `live_channels` or of `live_windows` on one device may be relied on, other than what follows from the above.
Results may differ from the reference program's by a relative error of at most 0.013.
Values may be sent and summed in bfloat16 or wider, within the bound.
No kernel may reach another device: no remote copies, remote signals or barrier semaphores. Data moves between devices by JAX's collectives and lax.ppermute only.
A program may use at most 128 MiB of HBM per device.

```python
import math
import jax
import jax.numpy as jnp
from jax import lax

BLOCK = 40
SAMPLES = 2048
BAND = 512
FIRST_BIN = 32
HALF = 64
LAGS = 512
NSHIFT = 2
W_DEV = 16
CHANNELS = 2560
WINDOWS = 64
N_CHAN = 64
N_HOUR = 4


def with_ends(values, key, smallest, top_value):
    index_at = [jax.random.randint(jax.random.fold_in(key, axis), (), 0, length) for axis, length in enumerate(values.shape)]
    longest = values.shape.index(max(values.shape))
    neighbour = index_at[:longest] + [(index_at[longest] + 1) % values.shape[longest]] + index_at[longest + 1:]
    return values.at[tuple(index_at)].set(smallest).at[tuple(neighbour)].set(top_value)


def levels(stream_key, dims, cuts, least, top_value):
    loudness, own = 1.0, jax.random.fold_in(stream_key, 6)
    for axis_at, blocks in cuts:
        steps = jnp.exp(jax.random.uniform(jax.random.fold_in(own, axis_at), (blocks,), jnp.float32, least / len(cuts), top_value / len(cuts)))
        loudness = loudness * jnp.repeat(steps, dims[axis_at] // blocks).reshape([-1 if axis == axis_at else 1 for axis in range(len(dims))])
    return loudness


def centred(rng, extent, width, reach, cuts=(), kind=jnp.bfloat16):
    values = width * jax.random.normal(rng, extent, jnp.float32)
    if cuts:
        values = values * levels(rng, extent, cuts, -0.22, 0.18)
    return jnp.clip(values, -reach, reach).astype(kind)


def setup_inputs(seed: int = 0) -> dict:
    streams_of = jax.random.split(jax.random.key(seed), 4)
    records = centred(streams_of[0], (CHANNELS, WINDOWS, SAMPLES), 1.0, 6.0, ((0, 64), (1, 4)))
    live_channels = with_ends((jax.random.randint(streams_of[1], (CHANNELS,), 0, 16) < 15).astype(jnp.int32), jax.random.fold_in(streams_of[1], 1), 0, 1)
    live_windows = with_ends((jax.random.randint(streams_of[2], (WINDOWS,), 0, 8) < 7).astype(jnp.int32), jax.random.fold_in(streams_of[2], 1), 0, 1)
    return {"records": records, "live_channels": live_channels, "live_windows": live_windows}


def forward_table():
    times = jnp.arange(SAMPLES, dtype=jnp.int32)[:, None]
    bins = FIRST_BIN + jnp.arange(BAND, dtype=jnp.int32)[None, :]
    phase = times * bins % SAMPLES
    angle = phase.astype(jnp.float32) * (2.0 * math.pi / SAMPLES)
    return jnp.concatenate([jnp.cos(angle), -jnp.sin(angle)], axis=1).astype(jnp.bfloat16)

def inverse_table():
    bins = FIRST_BIN + jnp.arange(BAND, dtype=jnp.int32)[:, None]
    shifts = jnp.arange(LAGS, dtype=jnp.int32)[None, :] - LAGS // 2
    phase = bins * shifts % SAMPLES
    angle = phase.astype(jnp.float32) * (2.0 * math.pi / SAMPLES)
    return jnp.concatenate([jnp.cos(angle), -jnp.sin(angle)], axis=0).astype(jnp.bfloat16)

def smoothing_matrix():
    index = jnp.arange(BAND, dtype=jnp.int32)
    inside = (jnp.abs(index[:, None] - index[None, :]) <= HALF).astype(jnp.float32)
    counts = lax.optimization_barrier(jnp.sum(inside, axis=0, keepdims=True))
    return inside / counts

def whiten(spectra, live_rows, smoother):
    real_part = spectra[:, :BAND]
    imag_part = spectra[:, BAND:]
    amplitude = jnp.sqrt(real_part * real_part + imag_part * imag_part)
    smooth = jnp.dot(amplitude, smoother, precision=lax.Precision.HIGHEST)
    factor = live_rows / (smooth + 1e-06)
    return jnp.concatenate([real_part * factor, imag_part * factor], axis=1).astype(jnp.bfloat16)

def cross_lags(own_spectra, other_spectra, inverse, norm_factor):
    own_real = own_spectra[..., :BAND].astype(jnp.float32)
    own_imag = own_spectra[..., BAND:].astype(jnp.float32)
    far_real = other_spectra[..., :BAND].astype(jnp.float32)
    far_imag = other_spectra[..., BAND:].astype(jnp.float32)

    def inner(left, right):
        return jnp.einsum('cwf,dwf->cdf', left, right)
    cross_real = inner(own_real, far_real) + inner(own_imag, far_imag)
    cross_imag = inner(own_real, far_imag) - inner(own_imag, far_real)
    stacked = jnp.concatenate([cross_real, cross_imag], axis=-1).astype(jnp.bfloat16)
    rows_here = stacked.shape[0] * stacked.shape[1]
    lagged = jnp.dot(stacked.reshape(rows_here, 2 * BAND).astype(jnp.float32), inverse.astype(jnp.float32))
    return (lagged * norm_factor).reshape(stacked.shape[0], stacked.shape[1], LAGS)

def reference(records, live_channels, live_windows):
    forward = forward_table().astype(jnp.float32)
    inverse = inverse_table()
    smoother = smoothing_matrix()
    norm_factor = 1.0 / math.sqrt(WINDOWS * BAND)
    window_live = live_windows.astype(jnp.float32)

    def spectra_of(operands):
        block_records, block_live = operands
        spectra = jnp.dot(block_records.reshape(BLOCK * WINDOWS, SAMPLES).astype(jnp.float32), forward)
        live_rows = (block_live.astype(jnp.float32)[:, None] * window_live[None, :]).reshape(BLOCK * WINDOWS, 1)
        return whiten(spectra, live_rows, smoother).reshape(BLOCK, WINDOWS, 2 * BAND)
    whitened = lax.map(spectra_of, (records.reshape(N_CHAN, BLOCK, WINDOWS, SAMPLES), live_channels.reshape(N_CHAN, BLOCK)))

    def correlate_block(block_index):
        own_spectra = whitened[block_index]

        def per_shift(shift_index):
            other_spectra = whitened[(block_index + shift_index + 1) % N_CHAN]

            def per_hour(hour_index):
                start = (hour_index * W_DEV).astype(jnp.int32)
                own_part = lax.dynamic_slice_in_dim(own_spectra, start, W_DEV, 1)
                far_part = lax.dynamic_slice_in_dim(other_spectra, start, W_DEV, 1)
                lagged = cross_lags(own_part, far_part, inverse, norm_factor)
                return lax.optimization_barrier(lagged.astype(jnp.bfloat16)).astype(jnp.float32)
            return lax.optimization_barrier(jnp.sum(lax.map(per_hour, jnp.arange(N_HOUR, dtype=jnp.int32)), axis=0))
        return lax.map(per_shift, jnp.arange(NSHIFT, dtype=jnp.int32))
    result = lax.map(correlate_block, jnp.arange(N_CHAN, dtype=jnp.int32))
    result = jnp.transpose(result, (0, 2, 1, 3, 4)).reshape(CHANNELS, NSHIFT, BLOCK, LAGS)
    return result.astype(jnp.bfloat16)
```

```python
import functools
import math

import jax
import jax.numpy as jnp
import ml_dtypes
import numpy as np
from jax import lax
from jax.experimental import pallas as pl
from jax.experimental.pallas import tpu as pltpu
from jax.sharding import PartitionSpec as P

SAMPLES = 2048
BAND = 512
FIRST_BIN = 32
HALF = 64
LAGS = 512
NSHIFT = 2
LANES = 128
GROUP = 8
UNROLL = 4
NT = (((1,), (1,)), ((), ()))
F32 = jnp.float32
BF16 = jnp.bfloat16
PARAMS = pltpu.CompilerParams(vmem_limit_bytes=60 << 20)


def passed_along(value, axis, steps):
    count = lax.axis_size(axis)
    return lax.ppermute(value, axis, [(s, (s + steps) % count) for s in range(count)])


def swapped(value, axis, bit):
    count = lax.axis_size(axis)
    return lax.ppermute(value, axis, [(s, s ^ bit) for s in range(count)])


def tables():
    bins = FIRST_BIN + np.arange(BAND)
    angle = (bins[:, None] * np.arange(SAMPLES)[None, :] % SAMPLES) * (2.0 * np.pi / SAMPLES)
    forward = np.concatenate([np.cos(angle), -np.sin(angle)], 0).astype(np.float32)
    shifts = np.arange(LAGS) - LAGS // 2
    angle = (bins[None, :] * shifts[:, None] % SAMPLES) * (2.0 * np.pi / SAMPLES)
    inverse = np.concatenate([np.cos(angle), -np.sin(angle)], 1).astype(np.float32)
    index = np.arange(BAND)
    inside = np.abs(index[:, None] - index[None, :]) <= HALF
    per_count = (1.0 / inside.sum(1, keepdims=True)).astype(np.float32)
    bf16 = ml_dtypes.bfloat16
    return forward.astype(bf16), inverse.astype(bf16), inside.astype(bf16), per_count


def whiten_body(records, forward, inside, per_count, live, out):
    spectra = lax.dot_general(forward[...], records[...], NT, preferred_element_type=F32)
    real, imag = spectra[:BAND], spectra[BAND:]
    amplitude = jnp.sqrt(real * real + imag * imag)
    high = amplitude.astype(BF16)
    low = (amplitude - high.astype(F32)).astype(BF16)
    total = jnp.dot(inside[...], high, preferred_element_type=F32)
    total = total + jnp.dot(inside[...], low, preferred_element_type=F32)
    factor = live[...] / (total * per_count[...] + 1e-06)
    out[:BAND, :] = (real * factor).astype(BF16)
    out[BAND:, :] = (imag * factor).astype(BF16)


def whitened(records, live, forward, inside, per_count):
    return pl.pallas_call(
        whiten_body,
        out_shape=jax.ShapeDtypeStruct((2 * BAND, records.shape[0]), BF16),
        compiler_params=PARAMS,
        name="whiten",
    )(records, forward, inside, per_count, live)


def cross_body(norm, own, left, right, inverse, give1, give2, keep1, keep2, near, far, cross):
    n_own, n_left, n_far = own.shape[1] // LANES, left.shape[1] // LANES, right.shape[1] // LANES
    n_near = n_own + n_left
    rows = 2 * BAND
    for q in range(n_own):
        near[q * rows : (q + 1) * rows, :] = own[:, q * LANES : (q + 1) * LANES].astype(F32)
    for q in range(n_left):
        base = (n_own + q) * rows
        near[base : base + rows, :] = left[:, q * LANES : (q + 1) * LANES].astype(F32)
    for m in range(n_far):
        far[m * rows : (m + 1) * rows, :] = right[:, m * LANES : (m + 1) * LANES].astype(F32)
    tile = (GROUP, LANES)
    windows = LANES // GROUP
    diagonal = lax.broadcasted_iota(jnp.int32, tile, 1) // windows == lax.broadcasted_iota(jnp.int32, tile, 0)
    zero = jnp.zeros(tile, F32)

    def turned(row):
        return pltpu.roll(jnp.broadcast_to(row, tile), 0, 1, stride=windows, stride_axis=0)

    def one_bin(f):
        halves = []
        for part in range(2):
            pieces = []
            for q in range(n_near):
                row = near[pl.ds(q * rows + part * BAND + f, 1), :]
                pieces.append(jnp.where(diagonal, jnp.broadcast_to(row, tile), zero))
            pieces += [zero] * (LANES // GROUP - n_near)
            halves.append(jnp.concatenate(pieces, 0).astype(BF16))
        near_rows = jnp.concatenate(halves, 1)
        first, second = [], []
        for m in range(n_far):
            real = turned(far[pl.ds(m * rows + f, 1), :])
            imag = turned(far[pl.ds(m * rows + BAND + f, 1), :])
            first += [real, imag]
            second += [imag, -real]
        far_rows = jnp.concatenate(
            [jnp.concatenate(first, 0).astype(BF16), jnp.concatenate(second, 0).astype(BF16)], 1
        )
        product = lax.dot_general(far_rows, near_rows, NT, preferred_element_type=F32)
        for m in range(n_far):
            for part in range(2):
                at = (2 * m + part) * GROUP
                cross[pl.ds(m * GROUP * rows + part * BAND + f, GROUP, stride=rows), :] = product[at : at + GROUP, :]

    def some_bins(step, carry):
        for u in range(UNROLL):
            one_bin(step * UNROLL + u)
        return carry

    lax.fori_loop(0, BAND // UNROLL, some_bins, 0)
    wo, wl = n_own * GROUP, n_left * GROUP
    half = LAGS // 2
    for pair in range(n_far * GROUP // 2):
        both = []
        for i in range(2):
            m, turn = divmod(2 * pair + i, GROUP)
            plane = m * GROUP + (GROUP - turn) % GROUP
            both.append(cross[plane * rows : (plane + 1) * rows, :].astype(BF16))
        lagged = jnp.dot(inverse[...], jnp.concatenate(both, 1), preferred_element_type=F32) * norm
        lagged = lagged.astype(BF16)
        for i in range(2):
            d = 2 * pair + i
            base = i * LANES
            give1[:, d * wo : (d + 1) * wo] = lagged[:half, base : base + wo]
            keep1[:, d * wo : (d + 1) * wo] = lagged[half:, base : base + wo]
            give2[:, d * wl : (d + 1) * wl] = lagged[:half, base + wo : base + wo + wl]
            keep2[:, d * wl : (d + 1) * wl] = lagged[half:, base + wo : base + wo + wl]


def cross_lags(own, left, right, inverse, norm):
    n_own, n_left, n_far = own.shape[1] // LANES, left.shape[1] // LANES, right.shape[1] // LANES
    first = jax.ShapeDtypeStruct((LAGS // 2, n_far * n_own * GROUP * GROUP), BF16)
    second = jax.ShapeDtypeStruct((LAGS // 2, n_far * n_left * GROUP * GROUP), BF16)
    rows = 2 * BAND
    return pl.pallas_call(
        functools.partial(cross_body, norm),
        out_shape=[first, second, first, second],
        scratch_shapes=[
            pltpu.VMEM(((n_own + n_left) * rows, LANES), F32),
            pltpu.VMEM((n_far * rows, LANES), F32),
            pltpu.VMEM((n_far * GROUP * rows, LANES), F32),
        ],
        compiler_params=PARAMS,
        name="cross",
    )(own, left, right, inverse)


def add_body(keep1, keep2, got1, got2, give1, give2):
    half = LAGS // 4
    give1[...] = (keep1[:half, :].astype(F32) + got1[:half, :].astype(F32)).astype(BF16)
    give2[...] = (keep2[:half, :].astype(F32) + got2[:half, :].astype(F32)).astype(BF16)


def added(keep1, keep2, got1, got2):
    shape = jax.ShapeDtypeStruct((LAGS // 4, keep1.shape[1]), BF16)
    return pl.pallas_call(add_body, out_shape=[shape, shape], compiler_params=PARAMS, name="add")(
        keep1, keep2, got1, got2
    )


def finish_body(keep1, keep2, got1, got2, last1, last2, out1, out2, turned):
    quarter = LAGS // 4
    block = out1.shape[0]
    pairs = block * block
    for keep, got, last, out in ((keep1, got1, last1, out1), (keep2, got2, last2, out2)):
        total = keep[quarter:, :].astype(F32) + got[quarter:, :].astype(F32) + last[...].astype(F32)
        turned[...] = jnp.transpose(total)
        for c in range(block):
            for m in range(block // GROUP):
                rows = turned[pl.ds(m * GROUP * block + c, GROUP, stride=block), :]
                rows = pltpu.roll(rows, c % GROUP, 0)
                out[c, m * GROUP : (m + 1) * GROUP, :] = rows.astype(BF16)


def finished(keep1, keep2, got1, got2, last1, last2, block):
    shape = jax.ShapeDtypeStruct((block, block, LAGS // 4), BF16)
    return pl.pallas_call(
        finish_body,
        out_shape=[shape, shape],
        scratch_shapes=[pltpu.VMEM((block * block, LAGS // 4), F32)],
        compiler_params=PARAMS,
        name="finish",
    )(keep1, keep2, got1, got2, last1, last2)


def local(records, live_channels, live_windows):
    channels_here, windows_here, samples_here = records.shape
    norm = 1.0 / math.sqrt(windows_here * lax.axis_size("hour") * BAND)
    forward, inverse, inside, per_count = tables()
    live = live_channels.astype(F32)[:, None] * live_windows.astype(F32)[None, :]
    hour = lax.axis_index("hour")
    quarters = jnp.asarray(inverse).reshape(4, LAGS // 4, 2 * BAND)
    inverse_here = jnp.concatenate(
        [lax.dynamic_index_in_dim(quarters, hour ^ bit, 0, keepdims=False) for bit in (3, 1, 2, 0)], 0
    )
    own = whitened(
        records.reshape(channels_here * windows_here, samples_here),
        live.reshape(1, channels_here * windows_here),
        forward,
        inside,
        per_count,
    )
    right = passed_along(own, "chan", -1)
    left = passed_along(own, "chan", 1)
    give1, give2, keep1, keep2 = cross_lags(own, left, right, inverse_here, norm)
    got1, got2 = swapped(give1, "hour", 1), swapped(give2, "hour", 1)
    send1, send2 = added(keep1, keep2, got1, got2)
    last1, last2 = swapped(send1, "hour", 2), swapped(send2, "hour", 2)
    out1, out2 = finished(keep1, keep2, got1, got2, last1, last2, channels_here)
    out2 = passed_along(out2, "chan", -1)
    return jnp.stack([out1, out2], axis=1)


def solution(mesh):
    placed = (P("chan", "hour", None), P("chan"), P("hour"))
    return jax.shard_map(
        local, mesh=mesh, in_specs=placed, out_specs=P("chan", None, None, "hour"), check_vma=False
    )
```

```python
import functools
import math

import jax
import jax.numpy as jnp
import ml_dtypes
import numpy as np
from jax import lax
from jax.experimental import pallas as pl
from jax.experimental.pallas import tpu as pltpu
from jax.sharding import PartitionSpec as P

SAMPLES = 2048
BAND = 512
FIRST_BIN = 32
HALF = 64
LAGS = 512
NSHIFT = 2
LANES = 128
GROUP = 8
UNROLL = 64
PAD_ROWS = 8
FIRST_GROUPS = 3
TABLE_PARTS = 4
CROSS_COST = 10_000_000_000
NT = (((1,), (1,)), ((), ()))
F32 = jnp.float32
BF16 = jnp.bfloat16
PARAMS = pltpu.CompilerParams(vmem_limit_bytes=64 << 20)
ANY = pl.BlockSpec(memory_space=pl.ANY)
SMEM = pl.BlockSpec(memory_space=pltpu.SMEM)
VMEM = pl.BlockSpec(memory_space=pltpu.VMEM)


def passed_along(value, axis, steps):
    count = lax.axis_size(axis)
    moved = lax.ppermute(value, axis, [(s, (s + steps) % count) for s in range(count)])
    return pltpu.with_memory_space_constraint(moved, pltpu.HBM)


def swapped(value, axis, bit):
    count = lax.axis_size(axis)
    moved = lax.ppermute(value, axis, [(s, s ^ bit) for s in range(count)])
    return pltpu.with_memory_space_constraint(moved, pltpu.HBM)


def tables():
    bins = FIRST_BIN + np.arange(BAND)
    angle = (bins[:, None] * np.arange(SAMPLES)[None, :] % SAMPLES) * (2.0 * np.pi / SAMPLES)
    forward = np.concatenate([np.cos(angle), -np.sin(angle)], 0).astype(np.float32)
    shifts = np.arange(LAGS) - LAGS // 2
    angle = (bins[None, :] * shifts[:, None] % SAMPLES) * (2.0 * np.pi / SAMPLES)
    inverse = np.concatenate([np.cos(angle), -np.sin(angle)], 1).astype(np.float32)
    index = np.arange(BAND)
    inside = np.abs(index[:, None] - index[None, :]) <= HALF
    per_count = (1.0 / inside.sum(1, keepdims=True)).astype(np.float32)
    bf16 = ml_dtypes.bfloat16
    return forward.astype(bf16), inverse.astype(bf16), inside.astype(bf16), per_count


def whiten_body(start, windows, channels, window_flags, per_count, inside, records, forward, out, rec, table, spec, sems):
    count = rec.shape[0]
    step = table.shape[0] // TABLE_PARTS
    copies = [pltpu.make_async_copy(records.at[pl.ds(start, count), :], rec, sems.at[TABLE_PARTS])]
    for part in range(TABLE_PARTS):
        rows = pl.ds(part * step, step)
        copies.append(pltpu.make_async_copy(forward.at[rows, :], table.at[rows, :], sems.at[part]))
    for copy in copies:
        copy.start()
    lane = lax.broadcasted_iota(jnp.int32, (1, count), 1)
    live_c = jnp.zeros((1, count), jnp.int32)
    for c in range(count // windows):
        live_c = jnp.where(lane // windows == c, channels[start // windows + c], live_c)
    live_w = jnp.zeros((1, count), jnp.int32)
    for w in range(windows):
        live_w = jnp.where(lane % windows == w, window_flags[w], live_w)
    live = live_c.astype(F32) * live_w.astype(F32)
    copies[0].wait()
    for part in range(TABLE_PARTS):
        copies[part + 1].wait()
        rows = slice(part * step, (part + 1) * step)
        spec[rows, :] = lax.dot_general(table[rows, :], rec[...], NT, preferred_element_type=F32)
    real, imag = spec[:BAND, :], spec[BAND:, :]
    amplitude = jnp.sqrt(real * real + imag * imag)
    high = amplitude.astype(BF16)
    low = (amplitude - high.astype(F32)).astype(BF16)
    total = jnp.dot(inside[...], high, preferred_element_type=F32)
    total = total + jnp.dot(inside[...], low, preferred_element_type=F32)
    factor = live / (total * per_count[...] + 1e-06)
    out[:BAND, :] = (real * factor).astype(BF16)
    out[BAND:, :] = (imag * factor).astype(BF16)


def whitened(records, channels, window_flags, start, count, forward, inside, per_count):
    windows = window_flags.shape[0]
    return pl.pallas_call(
        functools.partial(whiten_body, start, windows),
        out_shape=jax.ShapeDtypeStruct((2 * BAND, count), BF16),
        in_specs=[SMEM, SMEM, VMEM, VMEM, ANY, ANY],
        scratch_shapes=[
            pltpu.VMEM((count, records.shape[1]), BF16),
            pltpu.VMEM(forward.shape, BF16),
            pltpu.VMEM((2 * BAND, count), F32),
            pltpu.SemaphoreType.DMA((TABLE_PARTS + 1,)),
        ],
        compiler_params=PARAMS,
        cost_estimate=pl.CostEstimate(flops=CROSS_COST, transcendentals=0, bytes_accessed=4 << 20),
        name="whiten",
    )(channels, window_flags, per_count, inside, records, forward)


def lane_sets(n_near, n_far):
    per_set = LANES // (n_near * GROUP)
    sets, start = [], 0
    for first in range(0, n_far, per_set):
        groups = list(range(first, min(first + per_set, n_far)))
        wide = len(groups) * n_near * GROUP
        slot = LANES if wide > 96 else wide
        sets.append((groups, start, slot))
        start += slot * GROUP
    return sets, start


def widened(source, target):
    rows = source.shape[0]

    def some_rows(step, carry):
        at = pl.multiple_of(step * LANES, LANES)
        for q in range(source.shape[1] // LANES):
            target[pl.ds(q * rows + at, LANES), :] = source[pl.ds(at, LANES), q * LANES : (q + 1) * LANES].astype(F32)
        return carry

    lax.fori_loop(0, rows // LANES, some_rows, 0)


def cross_body(norm, n_right, *refs):
    give, keep, near_b, far_b, table, near, far, cross, lags, sems = refs[-10:]
    inverse, near_parts, far_parts = refs[0], refs[1:3], refs[3 : 3 + n_right]
    rows = 2 * BAND
    n_near, n_far = near_b.shape[1] // LANES, far_b.shape[1] // LANES
    sets, wide_all = lane_sets(n_near, n_far)
    loads = []
    for parts, target in ((far_parts, far_b), (near_parts, near_b)):
        start = 0
        for part in parts:
            columns = slice(start, start + part.shape[1])
            loads.append(pltpu.make_async_copy(part, target.at[:, columns], sems.at[len(loads)]))
            start += part.shape[1]
    loads.append(pltpu.make_async_copy(inverse, table, sems.at[len(loads)]))
    for load in loads:
        load.start()
    for load in loads[:n_right]:
        load.wait()
    widened(far_b, far)
    for load in loads[n_right:-1]:
        load.wait()
    widened(near_b, near)
    tile = (GROUP, LANES)
    windows = LANES // GROUP
    diagonal = lax.broadcasted_iota(jnp.int32, tile, 1) // windows == lax.broadcasted_iota(jnp.int32, tile, 0)
    zero = jnp.zeros(tile, F32)
    wide = n_near * GROUP
    pitch = rows + PAD_ROWS

    def turned(row):
        return pltpu.roll(jnp.broadcast_to(row, tile), 0, 1, stride=windows, stride_axis=0)

    def one_bin(f):
        halves = []
        for part in range(2):
            pieces = []
            for q in range(n_near):
                row = near[pl.ds(q * rows + part * BAND + f, 1), :]
                pieces.append(jnp.where(diagonal, jnp.broadcast_to(row, tile), zero))
            pieces += [zero] * (windows - n_near)
            halves.append(jnp.concatenate(pieces, 0).astype(BF16))
        near_rows = jnp.concatenate(halves, 1)
        first, second = [], []
        for m in range(n_far):
            real = turned(far[pl.ds(m * rows + f, 1), :])
            imag = turned(far[pl.ds(m * rows + BAND + f, 1), :])
            first += [real, imag]
            second += [imag, -real]
        far_rows = jnp.concatenate(
            [jnp.concatenate(first, 0).astype(BF16), jnp.concatenate(second, 0).astype(BF16)], 1
        )
        product = lax.dot_general(far_rows, near_rows, NT, preferred_element_type=F32)
        for number, (groups, _, _) in enumerate(sets):
            for part in range(2):
                total = None
                for i, m in enumerate(groups):
                    at = (2 * m + part) * GROUP
                    term = product[at : at + GROUP, :]
                    total = total + pltpu.roll(term, i * wide, 1) if i else term
                cross[pl.ds(number * GROUP * pitch + part * BAND + f, GROUP, stride=pitch), :] = total

    def some_bins(step, carry):
        for u in range(UNROLL):
            one_bin(step * UNROLL + u)
        return carry

    lax.fori_loop(0, BAND // UNROLL, some_bins, 0)
    half = LAGS // 2
    loads[-1].wait()
    for number, (_, first, slot) in enumerate(sets):

        def two_turns(step, carry):
            planes = []
            for i in range(2):
                plane = number * GROUP + (GROUP - 2 * step - i) % GROUP
                planes.append(cross[pl.ds(pl.multiple_of(plane * pitch, GROUP), rows), :].astype(BF16))
            lagged = jnp.dot(table[...], jnp.concatenate(planes, 1), preferred_element_type=F32) * norm
            at = pl.multiple_of(first + step * 2 * LANES, 2 * LANES)
            lags[:, pl.ds(at, 2 * LANES)] = lagged.astype(BF16)
            return carry

        lax.fori_loop(0, GROUP // 2, two_turns, 0)
        if slot < LANES:
            for turn in range(1, GROUP):
                at = first + turn * LANES
                lags[:, first + turn * slot : first + (turn + 1) * slot] = lags[:, at : at + slot]
    stores = []
    for side, out in enumerate((give, keep)):
        block = lags.at[pl.ds(side * half, half), :wide_all]
        stores.append(pltpu.make_async_copy(block, out, sems.at[side]))
        stores[side].start()
    for store in stores:
        store.wait()


def cross_lags(near, right, inverse, norm, after):
    n_near = sum(part.shape[1] for part in near) // LANES
    n_far = sum(part.shape[1] for part in right) // LANES
    sets, wide = lane_sets(n_near, n_far)
    shape = jax.ShapeDtypeStruct((LAGS // 2, wide), BF16)
    rows = 2 * BAND
    return pl.pallas_call(
        functools.partial(cross_body, norm, len(right)),
        out_shape=[shape, shape],
        in_specs=[ANY] * (1 + len(near) + len(right) + len(after)),
        out_specs=[ANY, ANY],
        scratch_shapes=[
            pltpu.VMEM((rows, n_near * LANES), BF16),
            pltpu.VMEM((rows, n_far * LANES), BF16),
            pltpu.VMEM(inverse.shape, BF16),
            pltpu.VMEM((n_near * rows, LANES), F32),
            pltpu.VMEM((n_far * rows, LANES), F32),
            pltpu.VMEM((len(sets) * GROUP * (rows + PAD_ROWS), LANES), F32),
            pltpu.VMEM((LAGS, len(sets) * GROUP * LANES), BF16),
            pltpu.SemaphoreType.DMA((len(near) + len(right) + 1,)),
        ],
        compiler_params=PARAMS,
        cost_estimate=pl.CostEstimate(flops=CROSS_COST, transcendentals=0, bytes_accessed=4 << 20),
        name="cross",
    )(inverse, *near, *right, *after)


def rows_of(term, first):
    quarter = LAGS // 4
    return pl.ds(first * quarter if term.shape[0] > quarter else 0, quarter)


def column_loads(terms, first, parts, sems):
    loads, start = [], 0
    for group in terms:
        wide = group[0].shape[1]
        for i, (term, column) in enumerate(group_columns(group, start)):
            target = parts.at[i, :, pl.ds(start, wide)]
            source = term.at[rows_of(term, first), pl.ds(column, wide)]
            loads.append(pltpu.make_async_copy(source, target, sems.at[len(loads)]))
        start += wide
    for load in loads:
        load.start()
    for load in loads:
        load.wait()


def group_columns(group, start):
    wide = group[0].shape[1]
    return [(term, start if term.shape[1] > wide else 0) for term in group]


def grouped(refs, counts):
    groups, at = [], 0
    for count in counts:
        groups.append(refs[at : at + count])
        at += count
    return groups


def sum_of(parts):
    total = parts[0].astype(F32)
    for i in range(1, parts.shape[0]):
        total = total + parts[i].astype(F32)
    return total


def add_body(first, counts, *refs):
    out, parts, total, sems = refs[-4:]
    column_loads(grouped(refs, counts), first, parts, sems)
    total[...] = sum_of(parts).astype(BF16)
    store = pltpu.make_async_copy(total, out, sems.at[0])
    store.start()
    store.wait()


def summed(terms, first, after):
    quarter, wide = LAGS // 4, sum(group[0].shape[1] for group in terms)
    counts = [len(group) for group in terms]
    return pl.pallas_call(
        functools.partial(add_body, first, counts),
        out_shape=jax.ShapeDtypeStruct((quarter, wide), BF16),
        in_specs=[ANY] * (sum(counts) + len(after)),
        out_specs=ANY,
        scratch_shapes=[
            pltpu.VMEM((counts[0], quarter, wide), BF16),
            pltpu.VMEM((quarter, wide), BF16),
            pltpu.SemaphoreType.DMA((sum(counts),)),
        ],
        compiler_params=PARAMS,
        name="add",
    )(*[term for group in terms for term in group], *after)


def finish_body(shift, counts, *refs):
    out, parts, turned, rows_out, sems = refs[-5:]
    block = out.shape[0]
    column_loads(grouped(refs, counts), 1, parts, sems)
    turned[...] = jnp.transpose(sum_of(parts))
    for groups, start, slot in lane_sets(block // GROUP, block // GROUP)[0]:
        for c in range(block):
            for i, m in enumerate(groups):
                rows = turned[pl.ds(start + i * block + c, GROUP, stride=slot), :]
                rows_out[c, m * GROUP : (m + 1) * GROUP, :] = pltpu.roll(rows, c % GROUP, 0).astype(BF16)
    copy = pltpu.make_async_copy(rows_out, out.at[:, shift, :, :], sems.at[0])
    copy.start()
    copy.wait()


def finished(terms, out, shape, shift, after):
    quarter, wide = LAGS // 4, sum(group[0].shape[1] for group in terms)
    counts = [len(group) for group in terms]
    kept = [] if out is None else [out]
    return pl.pallas_call(
        functools.partial(finish_body, shift, counts),
        out_shape=jax.ShapeDtypeStruct(shape, BF16),
        in_specs=[ANY] * (sum(counts) + len(kept) + len(after)),
        out_specs=ANY,
        scratch_shapes=[
            pltpu.VMEM((counts[0], quarter, wide), BF16),
            pltpu.VMEM((wide, quarter), F32),
            pltpu.VMEM((shape[0], shape[0], quarter), BF16),
            pltpu.SemaphoreType.DMA((sum(counts),)),
        ],
        input_output_aliases={sum(counts): 0} if kept else {},
        compiler_params=PARAMS,
        name="finish",
    )(*[term for group in terms for term in group], *kept, *after)


def local(records, live_channels, live_windows):
    block, windows, samples = records.shape
    norm = 1.0 / math.sqrt(windows * lax.axis_size("hour") * BAND)
    forward, inverse, inside, per_count = tables()
    hour = lax.axis_index("hour")
    quarters = jnp.asarray(inverse).reshape(4, LAGS // 4, 2 * BAND)
    inverse_here = jnp.concatenate(
        [lax.dynamic_index_in_dim(quarters, hour ^ bit, 0, keepdims=False) for bit in (3, 1, 2, 0)], 0
    )
    flat = records.reshape(block * windows, samples)
    own, left, right = [], [], []
    start = 0
    for groups in (FIRST_GROUPS, block // GROUP - FIRST_GROUPS):
        piece = whitened(flat, live_channels, live_windows, start, groups * LANES, forward, inside, per_count)
        right.append(passed_along(piece, "chan", -1))
        left.append(passed_along(piece, "chan", 1))
        own.append(piece)
        start += groups * LANES
    shape = (block, NSHIFT, block, LAGS // 4)

    def correlated(near, far, *after):
        give, keep = cross_lags(near, far, inverse_here, norm, after)
        return give, keep, swapped(give, "hour", 1)

    near_a = correlated(own, right[:1], own[1], left[0])
    far = correlated(left, right, near_a[0])
    send = summed([far[1:]], 0, [])
    last = swapped(send, "hour", 2)
    near_b = correlated(own, right[1:], send)
    total = summed([(*far[1:], last)], 1, [near_b[0]])
    moved = passed_along(total, "chan", -1)
    send = summed([near_a[1:], near_b[1:]], 0, [total])
    last = swapped(send, "hour", 2)
    out = finished([(*near_a[1:], last), (*near_b[1:], last)], None, shape, 0, [])
    return finished([(moved,)], out, shape, 1, [])


def solution(mesh):
    placed = (P("chan", "hour", None), P("chan"), P("hour"))
    return jax.shard_map(
        local, mesh=mesh, in_specs=placed, out_specs=P("chan", None, None, "hour"), check_vma=False
    )
```

```python
import functools
import math

import jax
import jax.numpy as jnp
import ml_dtypes
import numpy as np
from jax import lax
from jax.experimental import pallas as pl
from jax.experimental.pallas import tpu as pltpu
from jax.sharding import PartitionSpec as P

SAMPLES = 2048
BAND = 512
FIRST_BIN = 32
HALF = 64
LAGS = 512
NSHIFT = 2
LANES = 128
GROUP = 8
UNROLL = 64
PAD_ROWS = 8
FIRST_GROUPS = 3
TABLE_PARTS = 4
CROSS_COST = 10_000_000_000
NT = (((1,), (1,)), ((), ()))
F32 = jnp.float32
BF16 = jnp.bfloat16
PARAMS = pltpu.CompilerParams(vmem_limit_bytes=64 << 20)
ANY = pl.BlockSpec(memory_space=pl.ANY)
SMEM = pl.BlockSpec(memory_space=pltpu.SMEM)
VMEM = pl.BlockSpec(memory_space=pltpu.VMEM)


def passed_along(value, axis, steps):
    count = lax.axis_size(axis)
    moved = lax.ppermute(value, axis, [(s, (s + steps) % count) for s in range(count)])
    return pltpu.with_memory_space_constraint(moved, pltpu.HBM)


def swapped(value, axis, bit):
    count = lax.axis_size(axis)
    moved = lax.ppermute(value, axis, [(s, s ^ bit) for s in range(count)])
    return pltpu.with_memory_space_constraint(moved, pltpu.HBM)


def tables():
    bins = FIRST_BIN + np.arange(BAND)
    angle = (bins[:, None] * np.arange(SAMPLES)[None, :] % SAMPLES) * (2.0 * np.pi / SAMPLES)
    forward = np.concatenate([np.cos(angle), -np.sin(angle)], 0).astype(np.float32)
    shifts = np.arange(LAGS) - LAGS // 2
    angle = (bins[None, :] * shifts[:, None] % SAMPLES) * (2.0 * np.pi / SAMPLES)
    inverse = np.concatenate([np.cos(angle), -np.sin(angle)], 1).astype(np.float32)
    index = np.arange(BAND)
    inside = np.abs(index[:, None] - index[None, :]) <= HALF
    per_count = (1.0 / inside.sum(1, keepdims=True)).astype(np.float32)
    bf16 = ml_dtypes.bfloat16
    return forward.astype(bf16), inverse.astype(bf16), inside.astype(bf16), per_count


def whiten_body(start, windows, channels, window_flags, per_count, inside, records, forward, out, rec, table, spec, sems):
    count = rec.shape[0]
    step = table.shape[0] // TABLE_PARTS
    copies = [pltpu.make_async_copy(records.at[pl.ds(start, count), :], rec, sems.at[TABLE_PARTS])]
    for part in range(TABLE_PARTS):
        rows = pl.ds(part * step, step)
        copies.append(pltpu.make_async_copy(forward.at[rows, :], table.at[rows, :], sems.at[part]))
    for copy in copies:
        copy.start()
    lane = lax.broadcasted_iota(jnp.int32, (1, count), 1)
    live_c = jnp.zeros((1, count), jnp.int32)
    for c in range(count // windows):
        live_c = jnp.where(lane // windows == c, channels[start // windows + c], live_c)
    live_w = jnp.zeros((1, count), jnp.int32)
    for w in range(windows):
        live_w = jnp.where(lane % windows == w, window_flags[w], live_w)
    live = live_c.astype(F32) * live_w.astype(F32)
    copies[0].wait()
    for part in range(TABLE_PARTS):
        copies[part + 1].wait()
        rows = slice(part * step, (part + 1) * step)
        spec[rows, :] = lax.dot_general(table[rows, :], rec[...], NT, preferred_element_type=F32)
    real, imag = spec[:BAND, :], spec[BAND:, :]
    amplitude = jnp.sqrt(real * real + imag * imag)
    high = amplitude.astype(BF16)
    low = (amplitude - high.astype(F32)).astype(BF16)
    total = jnp.dot(inside[...], high, preferred_element_type=F32)
    total = total + jnp.dot(inside[...], low, preferred_element_type=F32)
    factor = live / (total * per_count[...] + 1e-06)
    out[:BAND, :] = (real * factor).astype(BF16)
    out[BAND:, :] = (imag * factor).astype(BF16)


def whitened(records, channels, window_flags, start, count, forward, inside, per_count):
    windows = window_flags.shape[0]
    return pl.pallas_call(
        functools.partial(whiten_body, start, windows),
        out_shape=jax.ShapeDtypeStruct((2 * BAND, count), BF16),
        in_specs=[SMEM, SMEM, VMEM, VMEM, ANY, ANY],
        scratch_shapes=[
            pltpu.VMEM((count, records.shape[1]), BF16),
            pltpu.VMEM(forward.shape, BF16),
            pltpu.VMEM((2 * BAND, count), F32),
            pltpu.SemaphoreType.DMA((TABLE_PARTS + 1,)),
        ],
        compiler_params=PARAMS,
        cost_estimate=pl.CostEstimate(flops=CROSS_COST, transcendentals=0, bytes_accessed=4 << 20),
        name="whiten",
    )(channels, window_flags, per_count, inside, records, forward)


def lane_sets(n_near, n_far):
    per_set = LANES // (n_near * GROUP)
    sets, start = [], 0
    for first in range(0, n_far, per_set):
        groups = list(range(first, min(first + per_set, n_far)))
        wide = len(groups) * n_near * GROUP
        slot = LANES if wide > 96 else wide
        sets.append((groups, start, slot))
        start += slot * GROUP
    return sets, start


def widened(source, target):
    rows = source.shape[0]

    def some_rows(step, carry):
        at = pl.multiple_of(step * LANES, LANES)
        for q in range(source.shape[1] // LANES):
            target[pl.ds(q * rows + at, LANES), :] = source[pl.ds(at, LANES), q * LANES : (q + 1) * LANES].astype(F32)
        return carry

    lax.fori_loop(0, rows // LANES, some_rows, 0)


def cross_body(norm, n_right, *refs):
    give, keep, near_b, far_b, table, near, far, cross, lags, sems = refs[-10:]
    inverse, near_parts, far_parts = refs[0], refs[1:3], refs[3 : 3 + n_right]
    rows = 2 * BAND
    n_near, n_far = near_b.shape[1] // LANES, far_b.shape[1] // LANES
    sets, wide_all = lane_sets(n_near, n_far)
    loads = []
    for parts, target in ((far_parts, far_b), (near_parts, near_b)):
        start = 0
        for part in parts:
            columns = slice(start, start + part.shape[1])
            loads.append(pltpu.make_async_copy(part, target.at[:, columns], sems.at[len(loads)]))
            start += part.shape[1]
    loads.append(pltpu.make_async_copy(inverse, table, sems.at[len(loads)]))
    for load in loads:
        load.start()
    for load in loads[:n_right]:
        load.wait()
    widened(far_b, far)
    for load in loads[n_right:-1]:
        load.wait()
    widened(near_b, near)
    tile = (GROUP, LANES)
    windows = LANES // GROUP
    diagonal = lax.broadcasted_iota(jnp.int32, tile, 1) // windows == lax.broadcasted_iota(jnp.int32, tile, 0)
    zero = jnp.zeros(tile, F32)
    wide = n_near * GROUP
    pitch = rows + PAD_ROWS

    def turned(row):
        return pltpu.roll(jnp.broadcast_to(row, tile), 0, 1, stride=windows, stride_axis=0)

    def one_bin(f):
        halves = []
        for part in range(2):
            pieces = []
            for q in range(n_near):
                row = near[pl.ds(q * rows + part * BAND + f, 1), :]
                pieces.append(jnp.where(diagonal, jnp.broadcast_to(row, tile), zero))
            pieces += [zero] * (windows - n_near)
            halves.append(jnp.concatenate(pieces, 0).astype(BF16))
        near_rows = jnp.concatenate(halves, 1)
        first, second = [], []
        for m in range(n_far):
            real = turned(far[pl.ds(m * rows + f, 1), :])
            imag = turned(far[pl.ds(m * rows + BAND + f, 1), :])
            first += [real, imag]
            second += [imag, -real]
        far_rows = jnp.concatenate(
            [jnp.concatenate(first, 0).astype(BF16), jnp.concatenate(second, 0).astype(BF16)], 1
        )
        product = lax.dot_general(far_rows, near_rows, NT, preferred_element_type=F32)
        for number, (groups, _, _) in enumerate(sets):
            for part in range(2):
                total = None
                for i, m in enumerate(groups):
                    at = (2 * m + part) * GROUP
                    term = product[at : at + GROUP, :]
                    total = total + pltpu.roll(term, i * wide, 1) if i else term
                cross[pl.ds(number * GROUP * pitch + part * BAND + f, GROUP, stride=pitch), :] = total

    def some_bins(step, carry):
        for u in range(UNROLL):
            one_bin(step * UNROLL + u)
        return carry

    lax.fori_loop(0, BAND // UNROLL, some_bins, 0)
    half = LAGS // 2
    loads[-1].wait()
    for number, (_, first, slot) in enumerate(sets):

        def two_turns(step, carry):
            planes = []
            for i in range(2):
                plane = number * GROUP + (GROUP - 2 * step - i) % GROUP
                planes.append(cross[pl.ds(pl.multiple_of(plane * pitch, GROUP), rows), :].astype(BF16))
            lagged = jnp.dot(table[...], jnp.concatenate(planes, 1), preferred_element_type=F32) * norm
            at = pl.multiple_of(first + step * 2 * LANES, 2 * LANES)
            lags[:, pl.ds(at, 2 * LANES)] = lagged.astype(BF16)
            return carry

        lax.fori_loop(0, GROUP // 2, two_turns, 0)
        if slot < LANES:
            for turn in range(1, GROUP):
                at = first + turn * LANES
                lags[:, first + turn * slot : first + (turn + 1) * slot] = lags[:, at : at + slot]
    stores = []
    for side, out in enumerate((give, keep)):
        block = lags.at[pl.ds(side * half, half), :wide_all]
        stores.append(pltpu.make_async_copy(block, out, sems.at[side]))
        stores[side].start()
    for store in stores:
        store.wait()


def cross_lags(near, right, inverse, norm, after):
    n_near = sum(part.shape[1] for part in near) // LANES
    n_far = sum(part.shape[1] for part in right) // LANES
    sets, wide = lane_sets(n_near, n_far)
    shape = jax.ShapeDtypeStruct((LAGS // 2, wide), BF16)
    rows = 2 * BAND
    return pl.pallas_call(
        functools.partial(cross_body, norm, len(right)),
        out_shape=[shape, shape],
        in_specs=[ANY] * (1 + len(near) + len(right) + len(after)),
        out_specs=[ANY, ANY],
        scratch_shapes=[
            pltpu.VMEM((rows, n_near * LANES), BF16),
            pltpu.VMEM((rows, n_far * LANES), BF16),
            pltpu.VMEM(inverse.shape, BF16),
            pltpu.VMEM((n_near * rows, LANES), F32),
            pltpu.VMEM((n_far * rows, LANES), F32),
            pltpu.VMEM((len(sets) * GROUP * (rows + PAD_ROWS), LANES), F32),
            pltpu.VMEM((LAGS, len(sets) * GROUP * LANES), BF16),
            pltpu.SemaphoreType.DMA((len(near) + len(right) + 1,)),
        ],
        compiler_params=PARAMS,
        cost_estimate=pl.CostEstimate(flops=CROSS_COST, transcendentals=0, bytes_accessed=4 << 20),
        name="cross",
    )(inverse, *near, *right, *after)


def rows_of(term, first):
    quarter = LAGS // 4
    return pl.ds(first * quarter if term.shape[0] > quarter else 0, quarter)


def column_loads(terms, first, parts, sems):
    loads, start = [], 0
    for group in terms:
        wide = group[0].shape[1]
        for i, (term, column) in enumerate(group_columns(group, start)):
            target = parts.at[i, :, pl.ds(start, wide)]
            source = term.at[rows_of(term, first), pl.ds(column, wide)]
            loads.append(pltpu.make_async_copy(source, target, sems.at[len(loads)]))
        start += wide
    for load in loads:
        load.start()
    for load in loads:
        load.wait()


def group_columns(group, start):
    wide = group[0].shape[1]
    return [(term, start if term.shape[1] > wide else 0) for term in group]


def grouped(refs, counts):
    groups, at = [], 0
    for count in counts:
        groups.append(refs[at : at + count])
        at += count
    return groups


def sum_of(parts):
    total = parts[0].astype(F32)
    for i in range(1, parts.shape[0]):
        total = total + parts[i].astype(F32)
    return total


def add_body(first, counts, *refs):
    out, parts, total, sems = refs[-4:]
    column_loads(grouped(refs, counts), first, parts, sems)
    total[...] = sum_of(parts).astype(BF16)
    store = pltpu.make_async_copy(total, out, sems.at[0])
    store.start()
    store.wait()


def summed(terms, first, after):
    quarter, wide = LAGS // 4, sum(group[0].shape[1] for group in terms)
    counts = [len(group) for group in terms]
    return pl.pallas_call(
        functools.partial(add_body, first, counts),
        out_shape=jax.ShapeDtypeStruct((quarter, wide), BF16),
        in_specs=[ANY] * (sum(counts) + len(after)),
        out_specs=ANY,
        scratch_shapes=[
            pltpu.VMEM((counts[0], quarter, wide), BF16),
            pltpu.VMEM((quarter, wide), BF16),
            pltpu.SemaphoreType.DMA((sum(counts),)),
        ],
        compiler_params=PARAMS,
        name="add",
    )(*[term for group in terms for term in group], *after)


def finish_body(shift, counts, *refs):
    out, parts, turned, rows_out, sems = refs[-5:]
    block = out.shape[0]
    column_loads(grouped(refs, counts), 1, parts, sems)
    total = sum_of(parts)
    base = 0
    for groups, start, slot in lane_sets(block // GROUP, block // GROUP)[0]:
        pitch = slot
        if slot == LANES:
            pitch = slot + GROUP
            for turn in range(GROUP):
                at = base + turn * pitch
                turned[at : at + slot, :] = jnp.transpose(total[:, start + turn * slot : start + (turn + 1) * slot])
        else:
            turned[base : base + slot * GROUP, :] = jnp.transpose(total[:, start : start + slot * GROUP])
        for c in range(block):
            for i, m in enumerate(groups):
                rows = turned[pl.ds(base + i * block + c, GROUP, stride=pitch), :]
                rows_out[c, m * GROUP : (m + 1) * GROUP, :] = pltpu.roll(rows, c % GROUP, 0).astype(BF16)
        base += pitch * GROUP
    copy = pltpu.make_async_copy(rows_out, out.at[:, shift, :, :], sems.at[0])
    copy.start()
    copy.wait()


def finished(terms, out, shape, shift, after):
    quarter, wide = LAGS // 4, sum(group[0].shape[1] for group in terms)
    counts = [len(group) for group in terms]
    kept = [] if out is None else [out]
    return pl.pallas_call(
        functools.partial(finish_body, shift, counts),
        out_shape=jax.ShapeDtypeStruct(shape, BF16),
        in_specs=[ANY] * (sum(counts) + len(kept) + len(after)),
        out_specs=ANY,
        scratch_shapes=[
            pltpu.VMEM((counts[0], quarter, wide), BF16),
            pltpu.VMEM((wide + 2 * GROUP * GROUP, quarter), F32),
            pltpu.VMEM((shape[0], shape[0], quarter), BF16),
            pltpu.SemaphoreType.DMA((sum(counts),)),
        ],
        input_output_aliases={sum(counts): 0} if kept else {},
        compiler_params=PARAMS,
        name="finish",
    )(*[term for group in terms for term in group], *kept, *after)


def local(records, live_channels, live_windows):
    block, windows, samples = records.shape
    norm = 1.0 / math.sqrt(windows * lax.axis_size("hour") * BAND)
    forward, inverse, inside, per_count = tables()
    hour = lax.axis_index("hour")
    quarters = jnp.asarray(inverse).reshape(4, LAGS // 4, 2 * BAND)
    inverse_here = jnp.concatenate(
        [lax.dynamic_index_in_dim(quarters, hour ^ bit, 0, keepdims=False) for bit in (3, 1, 2, 0)], 0
    )
    flat = records.reshape(block * windows, samples)
    own, left, right = [], [], []
    start = 0
    for groups in (FIRST_GROUPS, block // GROUP - FIRST_GROUPS):
        piece = whitened(flat, live_channels, live_windows, start, groups * LANES, forward, inside, per_count)
        right.append(passed_along(piece, "chan", -1))
        left.append(passed_along(piece, "chan", 1))
        own.append(piece)
        start += groups * LANES
    shape = (block, NSHIFT, block, LAGS // 4)

    def correlated(near, far, *after):
        give, keep = cross_lags(near, far, inverse_here, norm, after)
        return give, keep, swapped(give, "hour", 1)

    near_a = correlated(own, right[:1], own[1], left[0])
    far = correlated(left, right, near_a[0])
    send = summed([far[1:]], 0, [])
    last = swapped(send, "hour", 2)
    near_b = correlated(own, right[1:], send)
    total = summed([(*far[1:], last)], 1, [near_b[0]])
    moved = passed_along(total, "chan", -1)
    send = summed([near_a[1:], near_b[1:]], 0, [total])
    last = swapped(send, "hour", 2)
    out = finished([(*near_a[1:], last), (*near_b[1:], last)], None, shape, 0, [])
    return finished([(moved,)], out, shape, 1, [])


def solution(mesh):
    placed = (P("chan", "hour", None), P("chan"), P("hour"))
    return jax.shard_map(
        local, mesh=mesh, in_specs=placed, out_specs=P("chan", None, None, "hour"), check_vma=False
    )
```
